32 devices in a mesh: section: 2 (over core), tensor: 4 (over z), dp: 4 (over y, x).
Axes of the slice: x: 2, y: 2, z: 4, core: 2. Of those that a mesh axis runs over, the one named last changes fastest.
Arguments:
- block_input: bfloat16 [8, 256, 2048], P('dp'), may hold values from -6 to 6
- cotangent: bfloat16 [8, 256, 2048], P('dp'), may hold values from -6 to 6
- lengths: int32 [8], P('dp'), may hold values from 1 to 256, 1280 in all
- attn_norm: bfloat16 [2, 2048], P('section', 'dp'), may hold values from 0.5 to 1.5
- w_qkv: bfloat16 [2, 2048, 3, 2048], P('section', 'dp', None, 'tensor')
- w_out: bfloat16 [2, 2048, 2048], P('section', 'tensor', 'dp'), may hold values from -0.5 to 0.5
- mlp_norm: bfloat16 [2, 2048], P('section', 'dp'), may hold values from 0.5 to 1.5
- w_gate_up: bfloat16 [2, 2048, 2, 8192], P('section', 'dp', None, 'tensor'), may hold values from -0.125 to 0.125
- w_down: bfloat16 [2, 8192, 2048], P('section', 'tensor', 'dp'), may hold values from -0.0625 to 0.0625
Outputs:
- activations: bfloat16 [2, 8, 256, 2048], P('section', 'dp')
- input_grads: bfloat16 [2, 8, 256, 2048], P('section', 'dp')
- grad_attn_norm: float32 [2, 2048], P('section', 'dp')
- grad_qkv: float32 [2, 2048, 3, 2048], P('section', 'dp', None, 'tensor')
- grad_out: float32 [2, 2048, 2048], P('section', 'tensor', 'dp')
- grad_mlp_norm: float32 [2, 2048], P('section', 'dp')
- grad_gate_up: float32 [2, 2048, 2, 8192], P('section', 'dp', None, 'tensor')
- grad_down: float32 [2, 8192, 2048], P('section', 'tensor', 'dp')
The draws below stay inside these ranges and needn't reach their ends.
Inputs may be any that keep to these rules, and one draw needn't show every extreme that they name: lengths[n] counts the real tokens of sequence n, at positions 0 to lengths[n] - 1; the lengths sum to 1280 and the longest is exactly 256.
All inputs are finite; a program needn't handle non-finite values. No bound on the sum of `lengths` on one device may be relied on, other than what follows from the above.
Results may differ from the reference program's by a relative error of at most 0.02.
Values may be sent and summed in bfloat16 or wider, within the bound.
No kernel may reach another device: no remote copies, remote signals or barrier semaphores. Data moves between devices by JAX's collectives and lax.ppermute only.
A program may use at most 320 MiB of HBM per device.

```python
import math
import jax
import jax.numpy as jnp
import numpy as np
from jax import lax

D = 2048
HEAD_DIM = 64
FF = 8192
SEQLEN = 256
NSEQ = 8
N_SECTION = 2


def draw_w_qkv(key, part):
    first_key = jax.random.fold_in(jax.random.fold_in(key, 17), 0)
    shape = (2, D, 3, D)
    base = jnp.clip(jax.random.normal(first_key, shape, jnp.float32), -6.0, 6.0)
    return (base * (1.0 / D) ** 0.5).astype(jnp.bfloat16)


def strengthened(entries, key, source, target, shards_of, factor):
    def block_of(dim):
        return (jnp.arange(entries.shape[dim]) // (entries.shape[dim] // shards_of)).reshape((-1,) + (1,) * (entries.ndim - 1 - dim))

    one_side = jax.random.permutation(key, shards_of)[block_of(target)]
    other_side = (block_of(target) + shards_of // 2) % shards_of
    return jnp.where((block_of(source) == one_side) | (block_of(source) == other_side), factor * entries, entries)


def level_of(stream_key, extent, shards, least, high):
    level, own = 1.0, jax.random.fold_in(stream_key, 6)
    for dim, shards_of in shards:
        draws = jnp.exp(jax.random.uniform(jax.random.fold_in(own, dim), (shards_of,), jnp.float32, least / len(shards), high / len(shards)))
        level = level * jnp.repeat(draws, extent[dim] // shards_of).reshape([-1 if axis == dim else 1 for axis in range(len(extent))])
    return level


def profile(number_of, total, reach, lean):
    weights = [(1 << 20) // math.isqrt(grade ** lean) + 1 for grade in range(2, number_of + 1)]
    rest, holding = total - reach - (number_of - 1), [1] * (number_of - 1)
    while rest > 0:
        movable = [i for i in range(number_of - 1) if holding[i] < reach]
        whole, left = sum([weights[i] for i in movable]), rest
        for i in movable:
            addition = min(reach - holding[i], max(1, left * weights[i] // whole), rest)
            holding[i] = holding[i] + addition
            rest = rest - addition
    return np.array([reach] + holding)


def uneven_parts(stream_key, count, total, limit, slope):
    if count == 2:
        one = jax.random.randint(stream_key, (), max(1, total - limit), min(limit, total - 1) + 1)
        return jnp.stack([one, total - one])
    sizes = jnp.asarray(profile(count, total, limit, slope), jnp.int32)
    twos = (count - 1) // 2
    giver, taker = sizes[1:1 + 2 * twos:2], sizes[2:2 + 2 * twos:2]
    room = jnp.minimum(giver - 1, limit - taker)
    passed = jax.random.randint(jax.random.fold_in(stream_key, 1), (twos,), 0, 1 << 20) % (room + 1)
    sizes = sizes.at[1:1 + 2 * twos:2].set(giver - passed).at[2:2 + 2 * twos:2].set(taker + passed)
    return sizes[jax.random.permutation(jax.random.fold_in(stream_key, 2), count)]


def scatter_about(key, shape, spread, bound, shards=(), kind=jnp.bfloat16):
    values = spread * jax.random.normal(key, shape, jnp.float32)
    if shards:
        values = values * level_of(key, shape, shards, -0.22, 0.18)
    return jnp.clip(values, -bound, bound).astype(kind)


def noise_with(stream_key, dims, deviation, limit, cuts, heavy, kind=jnp.bfloat16):
    entries = deviation * jax.random.normal(stream_key, dims, jnp.float32)
    if cuts:
        entries = entries * level_of(stream_key, dims, cuts, -0.22, 0.18)
    return jnp.clip(strengthened(entries, jax.random.fold_in(stream_key, 3), *heavy), -limit, limit).astype(kind)


def setup_inputs(seed: int = 0) -> dict:
    arg_keys = jax.random.split(jax.random.key(seed), 10)
    return {
        "block_input": scatter_about(arg_keys[0], (NSEQ, SEQLEN, D), 1.0, 6.0, ((0, 4),)),
        "cotangent": noise_with(arg_keys[1], (NSEQ, SEQLEN, D), 1.0, 6.0, ((0, 4),), (0, 2, 4, 2.0)),
        "lengths": uneven_parts(arg_keys[2], NSEQ, NSEQ * SEQLEN * 5 // 8, SEQLEN, 2).astype(jnp.int32),
        "attn_norm": jnp.clip(1.0 + 0.1 * jax.random.normal(arg_keys[3], (N_SECTION, D), jnp.float32), 0.5, 1.5).astype(jnp.bfloat16),
        "w_qkv": draw_w_qkv(jax.random.fold_in(arg_keys[9], 71), 0),
        "w_out": scatter_about(arg_keys[5], (N_SECTION, D, D), (D // 16) ** -0.5, 0.5, ((0, 2), (1, 4), (2, 4))),
        "mlp_norm": jnp.clip(1.0 + 0.1 * jax.random.normal(arg_keys[6], (N_SECTION, D), jnp.float32), 0.5, 1.5).astype(jnp.bfloat16),
        "w_gate_up": scatter_about(arg_keys[7], (N_SECTION, D, 2, FF), D ** -0.5, 0.125, ((0, 2), (1, 4), (3, 4))),
        "w_down": scatter_about(arg_keys[8], (N_SECTION, FF, D), FF ** -0.5, 0.0625, ((0, 2), (1, 4), (2, 4))),
    }


EPSILON = 1e-05
THETA = 130000.0

def rotary(seq, half):
    position = jnp.arange(seq, dtype=jnp.float32)[:, None]
    exponent = jnp.arange(half, dtype=jnp.float32) * (-1.0 / half)
    angle = position * (THETA ** exponent)[None, :]
    return (jnp.cos(angle)[:, None, :], jnp.sin(angle)[:, None, :])

def rotate(values, cosine, sine):
    half = values.shape[-1] // 2
    front, back = (values[..., :half], values[..., half:])
    return jnp.concatenate([front * cosine - back * sine, back * cosine + front * sine], axis=-1)

def unrotate(grads, cosine, sine):
    half = grads.shape[-1] // 2
    front, back = (grads[..., :half], grads[..., half:])
    return jnp.concatenate([front * cosine + back * sine, back * cosine - front * sine], axis=-1)

def normalize(resid, gain):
    inverse = lax.rsqrt(lax.optimization_barrier(jnp.mean(resid * resid, axis=-1, keepdims=True)) + EPSILON)
    normed = resid * inverse
    return (normed, inverse, normed * gain.astype(jnp.float32))

def forward_parts(weights, inputs, length):
    gain_one, w_qkv, w_out, gain_two, w_gate_up, w_down = weights
    seq, width = inputs.shape
    local = w_qkv.shape[2]
    heads = local // HEAD_DIM
    units = w_gate_up.shape[2]
    scale = HEAD_DIM ** (-0.5)
    resid = inputs.astype(jnp.float32)
    normed_one, inverse_one, scaled_one = normalize(resid, gain_one)
    attn_in = scaled_one.astype(jnp.bfloat16)
    proj = jnp.dot(attn_in, w_qkv.reshape(width, 3 * local), preferred_element_type=jnp.float32)
    proj = proj.reshape(seq, 3, heads, HEAD_DIM)
    cosine, sine = rotary(seq, HEAD_DIM // 2)
    query = rotate(proj[:, 0], cosine, sine).astype(jnp.bfloat16)
    keys = rotate(proj[:, 1], cosine, sine).astype(jnp.bfloat16)
    values = proj[:, 2].astype(jnp.bfloat16)
    scores = jnp.einsum('qhd,khd->hqk', query.astype(jnp.float32), keys.astype(jnp.float32)) * scale
    position = jnp.arange(seq, dtype=jnp.int32)
    allowed = (position[None, :] <= position[:, None]) & (position[None, :] < length)
    masked = jnp.where(allowed[None], scores, -1e+30)
    top = lax.optimization_barrier(jnp.max(masked, axis=-1, keepdims=True))
    logsum = top + jnp.log(lax.optimization_barrier(jnp.sum(jnp.exp(masked - top), axis=-1, keepdims=True)))
    probs = jnp.where(allowed[None], jnp.exp(masked - logsum), 0.0).astype(jnp.bfloat16)
    attended = jnp.einsum('hqk,khd->qhd', probs.astype(jnp.float32), values.astype(jnp.float32))
    attended = attended.astype(jnp.bfloat16).reshape(seq, local)
    hidden = resid + jnp.dot(attended, w_out, preferred_element_type=jnp.float32)
    normed_two, inverse_two, scaled_two = normalize(hidden, gain_two)
    mlp_in = scaled_two.astype(jnp.bfloat16)
    pair = jnp.dot(mlp_in, w_gate_up.reshape(width, 2 * units), preferred_element_type=jnp.float32)
    pair = pair.reshape(seq, 2, units)
    gate, upper = (pair[:, 0], pair[:, 1])
    mixed = (jax.nn.silu(gate) * upper).astype(jnp.bfloat16)
    valid = (position < length)[:, None]
    output = jnp.where(valid, hidden + jnp.dot(mixed, w_down, preferred_element_type=jnp.float32), 0.0)
    return {'normed_one': normed_one, 'inverse_one': inverse_one, 'attn_in': attn_in, 'query': query, 'keys': keys, 'values': values, 'probs': probs, 'attended': attended, 'normed_two': normed_two, 'inverse_two': inverse_two, 'mlp_in': mlp_in, 'gate': gate, 'upper': upper, 'mixed': mixed, 'valid': valid, 'cosine': cosine, 'sine': sine, 'output': output.astype(jnp.bfloat16)}

def backward_parts(weights, inputs, length, upstream):
    gain_one, w_qkv, w_out, gain_two, w_gate_up, w_down = weights
    parts = forward_parts(weights, inputs, length)
    seq = inputs.shape[0]
    local = w_qkv.shape[2]
    heads = local // HEAD_DIM
    scale = HEAD_DIM ** (-0.5)
    grad_y = jnp.where(parts['valid'], upstream.astype(jnp.float32), 0.0)
    grad_yb = grad_y.astype(jnp.bfloat16)
    grad_down = jnp.dot(parts['mixed'].T, grad_yb, preferred_element_type=jnp.float32)
    grad_mixed = jnp.dot(grad_yb, w_down.T, preferred_element_type=jnp.float32)
    gate, upper = (parts['gate'], parts['upper'])
    sigma = jax.nn.sigmoid(gate)
    grad_gate = grad_mixed * upper * sigma * (1.0 + gate * (1.0 - sigma))
    grad_upper = grad_mixed * gate * sigma
    grad_pair = jnp.stack([grad_gate, grad_upper], axis=1).astype(jnp.bfloat16)
    grad_gate_up = jnp.einsum('ld,lcf->dcf', parts['mlp_in'].astype(jnp.float32), grad_pair.astype(jnp.float32))
    grad_mlp_in = jnp.einsum('lcf,dcf->ld', grad_pair.astype(jnp.float32), w_gate_up.astype(jnp.float32))
    grad_gain_two = lax.optimization_barrier(jnp.sum(grad_mlp_in * parts['normed_two'], axis=0))
    through_two = grad_mlp_in * gain_two.astype(jnp.float32)
    normed_two = parts['normed_two']
    grad_hidden = grad_y + parts['inverse_two'] * (through_two - normed_two * lax.optimization_barrier(jnp.mean(through_two * normed_two, axis=-1, keepdims=True)))
    grad_hb = grad_hidden.astype(jnp.bfloat16)
    grad_w_out = jnp.dot(parts['attended'].T, grad_hb, preferred_element_type=jnp.float32)
    grad_att = jnp.dot(grad_hb, w_out.T, preferred_element_type=jnp.float32).astype(jnp.bfloat16)
    grad_att = grad_att.reshape(seq, heads, HEAD_DIM).astype(jnp.float32)
    probs = parts['probs'].astype(jnp.float32)
    values = parts['values'].astype(jnp.float32)
    query = parts['query'].astype(jnp.float32)
    keys = parts['keys'].astype(jnp.float32)
    attended = parts['attended'].reshape(seq, heads, HEAD_DIM).astype(jnp.float32)
    grad_value = jnp.einsum('hqk,qhd->khd', probs, grad_att).astype(jnp.bfloat16)
    grad_probs = jnp.einsum('qhd,khd->hqk', grad_att, values)
    delta = jnp.einsum('qhd,qhd->hq', grad_att, attended)[..., None]
    grad_scores = (probs * (grad_probs - delta) * scale).astype(jnp.bfloat16).astype(jnp.float32)
    grad_query = unrotate(jnp.einsum('hqk,khd->qhd', grad_scores, keys), parts['cosine'], parts['sine']).astype(jnp.bfloat16)
    grad_key = unrotate(jnp.einsum('hqk,qhd->khd', grad_scores, query), parts['cosine'], parts['sine']).astype(jnp.bfloat16)
    grad_proj = jnp.stack([grad_query, grad_key, grad_value], axis=1).reshape(seq, 3, local)
    grad_w_qkv = jnp.einsum('ld,lcj->dcj', parts['attn_in'].astype(jnp.float32), grad_proj.astype(jnp.float32))
    grad_attn_in = jnp.einsum('lcj,dcj->ld', grad_proj.astype(jnp.float32), w_qkv.astype(jnp.float32))
    normed_one = parts['normed_one']
    grad_gain_one = lax.optimization_barrier(jnp.sum(grad_attn_in * normed_one, axis=0))
    through_one = grad_attn_in * gain_one.astype(jnp.float32)
    grad_input = grad_hidden + parts['inverse_one'] * (through_one - normed_one * lax.optimization_barrier(jnp.mean(through_one * normed_one, axis=-1, keepdims=True)))
    grads = (grad_gain_one, grad_w_qkv, grad_w_out, grad_gain_two, grad_gate_up, grad_down)
    return (grad_input.astype(jnp.bfloat16), grads)

def reference(block_input, cotangent, lengths, attn_norm, w_qkv, w_out, mlp_norm, w_gate_up, w_down):

    def layer(index):
        return (attn_norm[index], w_qkv[index], w_out[index], mlp_norm[index], w_gate_up[index], w_down[index])

    def run_forward(index, inputs):
        weights = layer(index)
        return lax.map(lambda pair: forward_parts(weights, pair[0], pair[1])['output'], (inputs, lengths))

    def run_backward(index, inputs, upstream):
        weights = layer(index)
        start = tuple((jnp.zeros(item.shape, jnp.float32) for item in weights))

        def step(total, triple):
            grad_in, grads = backward_parts(weights, triple[0], triple[1], triple[2])
            return (tuple((left + right for left, right in zip(total, grads))), grad_in)
        total, grad_inputs = lax.scan(step, start, (inputs, lengths, upstream))
        return (grad_inputs, total)
    first_out = run_forward(0, block_input)
    second_out = run_forward(1, first_out)
    second_grad, grads_two = run_backward(1, first_out, cotangent)
    first_grad, grads_one = run_backward(0, block_input, second_grad)
    stacked = [jnp.stack([left, right]) for left, right in zip(grads_one, grads_two)]
    return (jnp.stack([first_out, second_out]), jnp.stack([first_grad, second_grad]), stacked[0], stacked[1], stacked[2], stacked[3], stacked[4], stacked[5])
```

```python
import jax
import jax.numpy as jnp
from jax import lax
from jax.sharding import PartitionSpec as P

HEAD_DIM = 64
EPSILON = 1e-05
THETA = 130000.0
BF = jnp.bfloat16
F32 = jnp.float32


def swap(value, axis, bits):
    count = lax.axis_size(axis)
    return lax.ppermute(value, axis, [(source, source ^ bits) for source in range(count)])


def mm(left, right, dims):
    return lax.dot_general(left, right, (dims, ((), ())), preferred_element_type=F32)


def reduce_tokens(partial):
    sent = partial.astype(BF)
    half = sent[0].astype(F32)
    for c in range(1, sent.shape[0]):
        half = half + swap(sent[c], "section", c).astype(F32)
    half_b = half.astype(BF)
    total = half[0]
    for k in range(1, half.shape[0]):
        total = total + swap(half_b[k], "tensor", k).astype(F32)
    return total


def gather_tokens(own):
    row = jnp.stack([own] + [swap(own, "tensor", k) for k in range(1, lax.axis_size("tensor"))])
    return jnp.stack([row] + [swap(row, "section", c) for c in range(1, lax.axis_size("section"))])


def normalize(resid, gain):
    inverse = lax.rsqrt(jnp.mean(resid * resid, axis=-1, keepdims=True) + EPSILON)
    normed = resid * inverse
    return normed, inverse, (normed * gain).astype(BF)


def rotate(values, cosine, sine):
    half = values.shape[-1] // 2
    front, back = values[..., :half], values[..., half:]
    return jnp.concatenate([front * cosine - back * sine, back * cosine + front * sine], axis=-1)


def unrotate(grads, cosine, sine):
    half = grads.shape[-1] // 2
    front, back = grads[..., :half], grads[..., half:]
    return jnp.concatenate([front * cosine + back * sine, back * cosine - front * sine], axis=-1)


def attention(proj, cosine, sine, allowed):
    count, seq, _, heads, _ = proj.shape
    query = rotate(proj[:, :, 0], cosine, sine).astype(BF)
    keys = rotate(proj[:, :, 1], cosine, sine).astype(BF)
    values = proj[:, :, 2].astype(BF)
    scores = jnp.einsum("nqhd,nkhd->nhqk", query, keys, preferred_element_type=F32) * HEAD_DIM**-0.5
    masked = jnp.where(allowed, scores, -1e30)
    top = jnp.max(masked, axis=-1, keepdims=True)
    logsum = top + jnp.log(jnp.sum(jnp.exp(masked - top), axis=-1, keepdims=True))
    probs = jnp.where(allowed, jnp.exp(masked - logsum), 0.0).astype(BF)
    attended = jnp.einsum("nhqk,nkhd->nqhd", probs, values, preferred_element_type=F32).astype(BF)
    return query, keys, values, probs, attended


def attention_grad(saved, grad_att, cosine, sine):
    query, keys, values, probs, attended = saved
    grad_value = jnp.einsum("nhqk,nqhd->nkhd", probs, grad_att, preferred_element_type=F32).astype(BF)
    grad_probs = jnp.einsum("nqhd,nkhd->nhqk", grad_att, values, preferred_element_type=F32)
    delta = jnp.einsum("nqhd,nqhd->nhq", grad_att, attended, preferred_element_type=F32)[..., None]
    grad_scores = (probs.astype(F32) * (grad_probs - delta) * HEAD_DIM**-0.5).astype(BF)
    query_raw = jnp.einsum("nhqk,nkhd->nqhd", grad_scores, keys, preferred_element_type=F32)
    key_raw = jnp.einsum("nhqk,nqhd->nkhd", grad_scores, query, preferred_element_type=F32)
    grad_query = unrotate(query_raw, cosine, sine).astype(BF)
    grad_key = unrotate(key_raw, cosine, sine).astype(BF)
    return jnp.stack([grad_query, grad_key, grad_value], axis=2)


def per_device(block_input, cotangent, lengths, attn_norm, w_qkv, w_out, mlp_norm, w_gate_up, w_down):
    section, tensor = lax.axis_index("section"), lax.axis_index("tensor")
    cores, lanes = lax.axis_size("section"), lax.axis_size("tensor")
    micro, seq, width = block_input.shape
    count = micro // cores
    span = seq // lanes
    tokens = micro * seq

    def to_relative(value):
        blocks = value.reshape(cores, count, lanes, span, width)
        rows = []
        for c in range(cores):
            core = lax.dynamic_index_in_dim(blocks, section ^ c, 0, False)
            rows.append(jnp.stack([lax.dynamic_index_in_dim(core, tensor ^ k, 1, False) for k in range(lanes)]))
        return jnp.stack(rows).reshape(cores, lanes, count * span, width)

    def from_relative(value):
        blocks = value.reshape(cores, lanes, count, span, width)
        rows = []
        for c in range(cores):
            core = lax.dynamic_index_in_dim(blocks, section ^ c, 0, False)
            rows.append(jnp.stack([lax.dynamic_index_in_dim(core, tensor ^ k, 0, False) for k in range(lanes)], axis=1))
        return jnp.stack(rows).reshape(micro, seq, width)

    gains = jnp.stack([attn_norm[0], mlp_norm[0]])
    gains = lax.all_gather(lax.all_gather(gains, "dp", axis=1, tiled=True), "section", axis=0).astype(F32)

    def halves(shard, axis):
        shape = shard.shape
        split = shard.reshape(shape[:axis] + (cores, shape[axis] // cores) + shape[axis + 1 :])
        mine = lax.dynamic_index_in_dim(split, section, axis, False)
        other = lax.dynamic_index_in_dim(split, 1 - section, axis, False)
        return mine, swap(other, "section", 1)

    def layers_of(mine, got):
        return jnp.where(section == 0, mine, got), jnp.where(section == 0, got, mine)

    rows = w_qkv.shape[1]
    qkv = layers_of(*halves(w_qkv[0], 2))
    out = layers_of(*halves(w_out[0], 0))
    gate_up = layers_of(*halves(w_gate_up[0], 2))
    down = layers_of(*halves(w_down[0], 0))
    local = qkv[0].shape[2]
    units = gate_up[0].shape[2]
    heads = local // HEAD_DIM

    def gathered(layer):
        return (
            lax.all_gather(qkv[layer].reshape(rows, 3 * local), "dp", axis=0, tiled=True),
            lax.all_gather(out[layer], "dp", axis=1, tiled=True),
            lax.all_gather(gate_up[layer].reshape(rows, 2 * units), "dp", axis=0, tiled=True),
            lax.all_gather(down[layer], "dp", axis=1, tiled=True),
        )

    block = (jnp.arange(lanes, dtype=jnp.int32) ^ tensor)[:, None, None]
    step = jnp.arange(span, dtype=jnp.int32)[None, None, :]
    position = jnp.broadcast_to(block * span + step, (lanes, count, span))
    own_lengths = lengths.reshape(cores, count)
    limit = jnp.stack([lax.dynamic_index_in_dim(own_lengths, section ^ c, 0, False) for c in range(cores)])
    valid = position[None] < limit[:, None, :, None]
    valid = valid.reshape(cores, lanes, count * span, 1)
    flat = position.transpose(1, 0, 2).reshape(count, seq)
    allowed = (flat[None, :, None, :] <= flat[None, :, :, None]) & (flat[None, :, None, :] < limit[:, :, None, None])
    allowed = allowed.reshape(micro, 1, seq, seq)
    exponent = jnp.arange(HEAD_DIM // 2, dtype=F32) * (-2.0 / HEAD_DIM)
    angle = flat.astype(F32)[:, :, None] * (THETA**exponent)
    cosine = jnp.tile(jnp.cos(angle), (cores, 1, 1))[:, :, None, :]
    sine = jnp.tile(jnp.sin(angle), (cores, 1, 1))[:, :, None, :]

    def per_sequence(value):
        inner = value.shape[1:]
        value = value.reshape((cores, lanes, count, span) + inner)
        return value.swapaxes(1, 2).reshape((micro, seq) + inner)

    def per_token(value):
        inner = value.shape[2:]
        value = value.reshape((cores, count, lanes, span) + inner)
        return value.swapaxes(1, 2).reshape((tokens,) + inner)

    def forward(layer, weights, inputs):
        w_qkv, w_out, w_gate_up, w_down = weights
        resid = inputs.astype(F32)
        _, _, attn_in = normalize(resid, gains[layer, 0])
        attn_in = attn_in.reshape(tokens, width)
        proj = mm(attn_in, w_qkv, ((1,), (0,))).reshape(tokens, 3, heads, HEAD_DIM)
        saved = attention(per_sequence(proj), cosine, sine, allowed)
        attended = per_token(saved[-1]).reshape(tokens, local)
        part = mm(attended, w_out, ((1,), (0,)))
        own = resid[0, 0]
        hidden = own + reduce_tokens(part.reshape(inputs.shape))
        normed_two, inverse_two, own_mlp_in = normalize(hidden, gains[layer, 1])
        mlp_in = gather_tokens(own_mlp_in).reshape(tokens, width)
        pair = mm(mlp_in, w_gate_up, ((1,), (0,)))
        gate, upper = pair[:, :units], pair[:, units:]
        mixed = (jax.nn.silu(gate) * upper).astype(BF)
        part = mm(mixed, w_down, ((1,), (0,)))
        output = jnp.where(valid[0, 0], hidden + reduce_tokens(part.reshape(inputs.shape)), 0.0).astype(BF)
        normed_one, inverse_one, _ = normalize(own, gains[layer, 0])
        keep = (attn_in, saved, attended, normed_one, inverse_one, normed_two, inverse_two, mlp_in, gate, upper, mixed)
        return gather_tokens(output), keep

    def scatter(value, axis):
        return lax.psum_scatter(value.astype(BF), "dp", scatter_dimension=axis, tiled=True)

    def backward(layer, weights, keep, upstream):
        w_qkv, w_out, w_gate_up, w_down = weights
        attn_in, saved, attended, normed_one, inverse_one, normed_two, inverse_two, mlp_in, gate, upper, mixed = keep
        grad_y = jnp.where(valid, upstream, jnp.zeros_like(upstream))
        grad_yb = grad_y.reshape(tokens, width)
        grad_down = scatter(mm(mixed, grad_yb, ((0,), (0,))), 1)
        grad_mixed = mm(grad_yb, w_down, ((1,), (1,)))
        sigma = jax.nn.sigmoid(gate)
        grad_gate = grad_mixed * upper * sigma * (1.0 + gate * (1.0 - sigma))
        grad_upper = grad_mixed * gate * sigma
        grad_pair = jnp.concatenate([grad_gate, grad_upper], axis=1).astype(BF)
        part = mm(grad_pair, w_gate_up, ((1,), (1,)))
        grad_gate_up = scatter(mm(mlp_in, grad_pair, ((0,), (0,))), 0)
        grad_mlp_in = reduce_tokens(part.reshape(upstream.shape))
        grad_gain_two = jnp.sum(grad_mlp_in * normed_two, axis=0)
        through = grad_mlp_in * gains[layer, 1]
        grad_hidden = grad_y[0, 0].astype(F32) + inverse_two * (
            through - normed_two * jnp.mean(through * normed_two, axis=-1, keepdims=True)
        )
        grad_hb = gather_tokens(grad_hidden.astype(BF)).reshape(tokens, width)
        grad_att = mm(grad_hb, w_out, ((1,), (1,))).astype(BF)
        grad_out = scatter(mm(attended, grad_hb, ((0,), (0,))), 1)
        grad_att = per_sequence(grad_att.reshape(tokens, heads, HEAD_DIM))
        grad_proj = attention_grad(saved, grad_att, cosine, sine)
        grad_proj = per_token(grad_proj).reshape(tokens, 3 * local)
        part = mm(grad_proj, w_qkv, ((1,), (1,)))
        grad_qkv = scatter(mm(attn_in, grad_proj, ((0,), (0,))), 0)
        grad_attn_in = reduce_tokens(part.reshape(upstream.shape))
        grad_gain_one = jnp.sum(grad_attn_in * normed_one, axis=0)
        through = grad_attn_in * gains[layer, 0]
        grad_input = grad_hidden + inverse_one * (
            through - normed_one * jnp.mean(through * normed_one, axis=-1, keepdims=True)
        )
        grads = (grad_qkv, grad_out, grad_gate_up, grad_down)
        return gather_tokens(grad_input.astype(BF)), grads, jnp.stack([grad_gain_one, grad_gain_two])

    weights = (gathered(0), gathered(1))
    first_out, keep_one = forward(0, weights[0], to_relative(block_input))
    second_out, keep_two = forward(1, weights[1], first_out)
    second_grad, grads_two, gain_grads_two = backward(1, weights[1], keep_two, to_relative(cotangent))
    first_grad, grads_one, gain_grads_one = backward(0, weights[0], keep_one, second_grad)

    activations = from_relative(jnp.where(section == 0, first_out, second_out))[None]
    input_grads = from_relative(jnp.where(section == 0, first_grad, second_grad))[None]

    gain_grads = lax.psum(jnp.stack([gain_grads_one, gain_grads_two]), ("section", "tensor", "dp"))
    gain_grads = lax.dynamic_index_in_dim(gain_grads, section, 0, False)
    gain_grads = lax.dynamic_slice_in_dim(gain_grads, lax.axis_index("dp") * rows, rows, 1)

    def joined(one, two, axis):
        own = jnp.where(section == 0, one, two)
        got = swap(jnp.where(section == 0, two, one), "section", 1)
        low, high = jnp.where(section == 0, own, got), jnp.where(section == 0, got, own)
        return jnp.concatenate([low, high], axis=axis).astype(F32)[None]

    shape_qkv, shape_pair = (rows, 3, local), (rows, 2, units)
    return (
        activations,
        input_grads,
        gain_grads[0][None],
        joined(grads_one[0].reshape(shape_qkv), grads_two[0].reshape(shape_qkv), 2),
        joined(grads_one[1], grads_two[1], 0),
        gain_grads[1][None],
        joined(grads_one[2].reshape(shape_pair), grads_two[2].reshape(shape_pair), 2),
        joined(grads_one[3], grads_two[3], 0),
    )


def solution(mesh):
    return jax.shard_map(
        per_device,
        mesh=mesh,
        in_specs=(
            P("dp", None, None),
            P("dp", None, None),
            P("dp"),
            P("section", "dp"),
            P("section", "dp", None, "tensor"),
            P("section", "tensor", "dp"),
            P("section", "dp"),
            P("section", "dp", None, "tensor"),
            P("section", "tensor", "dp"),
        ),
        out_specs=(
            P("section", "dp", None, None),
            P("section", "dp", None, None),
            P("section", "dp"),
            P("section", "dp", None, "tensor"),
            P("section", "tensor", "dp"),
            P("section", "dp"),
            P("section", "dp", None, "tensor"),
            P("section", "tensor", "dp"),
        ),
        check_vma=False,
    )
```
